512 devices in a mesh: dp: 4 (over x), expert: 128 (over z, y, core).
Axes of the slice: x: 4, y: 8, z: 8, core: 2. Of those that a mesh axis runs over, the one named last changes fastest.
Arguments:
- tokens: bfloat16 [8192, 2048], P(('dp', 'expert')), may hold values from -6 to 6
- cotangent: bfloat16 [8192, 2048], P(('dp', 'expert')), may hold values from -6 to 6
- routes: int32 [8192, 8], P(('dp', 'expert')), may hold values from 0 to 127, all different within a row; in each aligned block of 16 rows (0 to 15, 16 to 31, ...) at most 2 rows name the same one
- gate_values: float32 [8192, 8], P(('dp', 'expert')), may hold values from 0.1 to 1
- gate_weight: bfloat16 [128, 768, 2048], P('expert', 'dp'), may hold values from -0.125 to 0.125
- up_weight: bfloat16 [128, 768, 2048], P('expert', 'dp'), may hold values from -0.125 to 0.125
- down_weight: bfloat16 [128, 768, 2048], P('expert', None, 'dp'), may hold values from -0.21875 to 0.21875
Outputs:
- mixed: bfloat16 [8192, 2048], P(('dp', 'expert'))
- grad_gate_weight: bfloat16 [128, 768, 2048], P('expert', 'dp')
- grad_up_weight: bfloat16 [128, 768, 2048], P('expert', 'dp')
- grad_down_weight: bfloat16 [128, 768, 2048], P('expert', None, 'dp')
The draws below stay inside these ranges and needn't reach their ends.
Inputs may be any that keep to these rules, and one draw needn't show every extreme that they name: `routes`: each row names 8 different experts. Among the rows of one device no expert is named more than 2 times, and in some device's rows some expert is named exactly 2 times.
All inputs are finite; a program needn't handle non-finite values.
Results may differ from the reference program's by a relative error of at most 0.0058.
Values may be sent and summed in bfloat16 or wider, within the bound.
A program may use at most 64 MiB of HBM per device.

```python
import math
import jax
import jax.numpy as jnp
import numpy as np
from jax import lax

D = 2048
I = 768
TOP = 8
TOK_DEV = 16
EXPERTS = 128
CAP = 2
SLOTS = 1024
TOKENS = 8192


def levels(key, shape, cuts, least, largest):
    level = 1.0
    for axis_at, shards_of in cuts:
        steps = jax.random.uniform(jax.random.fold_in(jax.random.fold_in(key, 6), axis_at), (shards_of,), jnp.float32, least / len(cuts), largest / len(cuts))
        level = level * jnp.repeat(jnp.exp(steps), shape[axis_at] // shards_of).reshape((-1,) + (1,) * (len(shape) - 1 - axis_at))
    return level


def deal_out(own_key, own, number, rows, number_of, top, reach, skew):
    ranking = jax.random.permutation(own_key, number_of)
    crowded, ordinary = load_shares(number_of, rows * top, reach, skew, True), load_shares(number_of, rows * top, reach, skew, False)
    places = jnp.arange(number_of)

    def named(lengths, turn):
        used = int((lengths > 0).sum())
        fixed = max(1, used // 4)
        moved = fixed + (places - fixed + turn * (used - fixed)) % max(1, number_of - fixed)
        return jnp.zeros((number_of,), jnp.int32).at[ranking[jnp.where(places < fixed, places, moved)]].set(jnp.asarray(lengths, jnp.int32))

    lengths = jnp.where(number % 4 == 0, named(crowded, number // 4), named(ordinary, number - number // 4 - 1))
    mixed = jax.random.permutation(jax.random.fold_in(own, 3), number_of)
    giver, sink = mixed[0:number_of // 2 * 2:2], mixed[1:number_of // 2 * 2:2]
    slack = jnp.minimum(lengths[giver] - 1, reach - lengths[sink]) // 2
    slack = jnp.where((giver == ranking[0]) | (sink == ranking[0]) | (lengths[sink] == 0), 0, jnp.maximum(slack, 0))
    moved = jax.random.randint(jax.random.fold_in(own, 4), (number_of // 2,), 0, 1 << 20) % (slack + 1)
    lengths = lengths.at[giver].add(-moved).at[sink].add(moved)
    labels = jnp.searchsorted(jnp.cumsum(lengths), jnp.arange(rows * top), side="right").astype(jnp.int32)
    table = labels.reshape(top, rows).T
    table = table[jax.random.permutation(jax.random.fold_in(own, 1), rows)]
    turn = jax.random.randint(jax.random.fold_in(own, 2), (rows, 1), 0, top)
    return jnp.take_along_axis(table, (jnp.arange(top)[None, :] + turn) % top, axis=1)


def load_shares(amount, total, bound, slope, full):
    loads = [(1 << 20) // math.isqrt(grade ** slope) + 1 for grade in range(1, amount + 1)]
    largest = bound if full else min(bound, max(-(-total // amount), total * loads[0] // sum(loads)))
    least = 1 if total - largest >= amount - 1 else 0
    holding, rest = [largest] + [least] * (amount - 1), total - largest - least * (amount - 1)
    while rest > 0:
        free = [i for i in range(1, amount) if holding[i] < largest] or [i for i in range(1, amount) if holding[i] < bound]
        mass, remaining = sum([loads[i] for i in free]), rest
        for i in free:
            more = min(bound - holding[i], max(1, remaining * loads[i] // mass), rest)
            holding[i] = holding[i] + more
            rest = rest - more
    return np.array(holding)


def scatter_about(rng, extent, spread, bound, pieces=(), held_as=jnp.bfloat16):
    loudness = levels(rng, extent, pieces, -0.22, 0.18) if pieces else 1.0
    values = jax.random.normal(rng, extent, jnp.float32) * spread * loudness
    return jnp.minimum(jnp.maximum(values, -bound), bound).astype(held_as)


def setup_inputs(seed: int = 0) -> dict:
    keys = jax.random.split(jax.random.key(seed), 8)
    tokens = scatter_about(keys[0], (TOKENS, D), 1.0, 6.0, ((0, 512),))
    cotangent = scatter_about(keys[1], (TOKENS, D), 1.0, 6.0, ((0, 512),))
    routes_keys = jax.random.split(jax.random.fold_in(keys[2], 1), TOKENS // TOK_DEV)
    routes_turns = jax.random.permutation(jax.random.fold_in(keys[2], 3), TOKENS // TOK_DEV)
    routes = jax.vmap(lambda own, number: deal_out(jax.random.fold_in(keys[2], 2), own, number, TOK_DEV, EXPERTS, TOP, CAP, 2))(routes_keys, routes_turns).reshape((TOKENS, TOP))
    gate_values = jnp.clip(jnp.exp(math.log(1.0) - 2.3025851 * jax.random.uniform(keys[3], (TOKENS, TOP), jnp.float32) ** levels(keys[3], (TOKENS, TOP), ((0, 512),), -0.2, 0.2)), 0.1, 1.0)
    gate_weight = scatter_about(keys[4], (EXPERTS, I, D), D ** -0.5, 0.125, ((0, 128), (1, 4)))
    up_weight = scatter_about(keys[5], (EXPERTS, I, D), D ** -0.5, 0.125, ((0, 128), (1, 4)))
    down_weight = scatter_about(keys[6], (EXPERTS, I, D), I ** -0.5, 0.21875, ((0, 128), (2, 4)))
    return dict(tokens=tokens, cotangent=cotangent, routes=routes, gate_values=gate_values, gate_weight=gate_weight, up_weight=up_weight, down_weight=down_weight)


def reference(tokens, cotangent, routes, gate_values, gate_weight, up_weight, down_weight):
    devices = TOKENS // TOK_DEV
    onehot = routes[:, :, None] == jnp.arange(EXPERTS, dtype=jnp.int32)[None, None, :]
    named = jnp.sum(onehot.astype(jnp.int32), axis=1)
    blocks = named.reshape(devices, TOK_DEV, EXPERTS)
    earlier = (jnp.cumsum(blocks, axis=1) - blocks).reshape(TOKENS, EXPERTS)
    source = jnp.arange(TOKENS, dtype=jnp.int32) // TOK_DEV
    slot_row = (source[:, None] * CAP + earlier).astype(jnp.int32)
    token_gate = jnp.sum(jnp.where(onehot, gate_values[:, :, None], jnp.zeros((), jnp.float32)), axis=1)
    token_ids = jnp.arange(TOKENS, dtype=jnp.int32)

    def one_expert(mixed_sum, packed):
        named_col, row_col, gate_col, w_gate, w_up, w_down = packed
        target = jnp.where(named_col == 1, row_col, SLOTS).astype(jnp.int32)
        owner = jnp.zeros((SLOTS + 1,), jnp.int32).at[target].set(token_ids)[:SLOTS]
        live = jnp.zeros((SLOTS + 1,), jnp.int32).at[target].set(named_col)[:SLOTS]
        weight = jnp.zeros((SLOTS + 1,), jnp.float32).at[target].set(gate_col)[:SLOTS]
        expert_in = jnp.where(live[:, None] == 1, tokens[owner], jnp.zeros((), tokens.dtype))
        expert_cot = (weight[:, None] * cotangent[owner].astype(jnp.float32)).astype(jnp.bfloat16)
        gate = jnp.dot(expert_in, w_gate.T, preferred_element_type=jnp.float32)
        up = jnp.dot(expert_in, w_up.T, preferred_element_type=jnp.float32)
        hidden = (jax.nn.silu(gate) * up).astype(jnp.bfloat16)
        expert_out = jnp.dot(hidden, w_down, preferred_element_type=jnp.float32).astype(jnp.bfloat16)
        grad_down = jnp.dot(hidden.T, expert_cot, preferred_element_type=jnp.float32).astype(jnp.bfloat16)
        grad_hidden = jnp.dot(expert_cot, w_down.T, preferred_element_type=jnp.float32)
        sigma = jax.nn.sigmoid(gate)
        grad_gate = (grad_hidden * up * sigma * (1.0 + gate * (1.0 - sigma))).astype(jnp.bfloat16)
        grad_up = (grad_hidden * jax.nn.silu(gate)).astype(jnp.bfloat16)
        grad_gate_w = jnp.dot(grad_gate.T, expert_in, preferred_element_type=jnp.float32).astype(jnp.bfloat16)
        grad_up_w = jnp.dot(grad_up.T, expert_in, preferred_element_type=jnp.float32).astype(jnp.bfloat16)
        mixed_sum = mixed_sum.at[owner].add(weight[:, None] * expert_out.astype(jnp.float32))
        return mixed_sum, (grad_gate_w, grad_up_w, grad_down)

    start = jnp.zeros((TOKENS, D), jnp.float32)
    mixed_sum, grads = lax.scan(one_expert, start, (named.T, slot_row.T, token_gate.T, gate_weight, up_weight, down_weight))
    return mixed_sum.astype(jnp.bfloat16), grads[0], grads[1], grads[2]
```

```python
import jax
import jax.numpy as jnp
from jax import lax
from jax.sharding import PartitionSpec as P


def placement(routes, gate_values, experts, capacity):
    onehot = routes[:, :, None] == jnp.arange(experts, dtype=jnp.int32)[None, None, :]
    named = jnp.sum(onehot.astype(jnp.int32), axis=1)
    earlier = jnp.cumsum(named, axis=0) - named
    slot_ids = jnp.arange(capacity, dtype=jnp.int32)[None, :, None]
    placer = (named.T[:, None, :] == 1) & (earlier.T[:, None, :] == slot_ids)
    token_gate = jnp.sum(
        jnp.where(onehot, gate_values[:, :, None], jnp.zeros((), jnp.float32)), axis=1
    )
    slot_gate = jnp.sum(placer.astype(jnp.float32) * token_gate.T[:, None, :], axis=2)
    return placer, slot_gate


def body(tokens, cotangent, routes, gate_values, gate_weight, up_weight, down_weight):
    tok_rows = tokens.shape[0]
    width = tokens.shape[1]
    top_count = routes.shape[1]
    experts = lax.axis_size("expert")
    groups = lax.axis_size("dp")
    quarter = width // groups
    capacity = min(tok_rows, max(2, 2 * tok_rows * top_count // experts))

    placer, _ = placement(routes, gate_values, experts, capacity)
    row_input = jnp.einsum(
        "est,td->esd", placer.astype(jnp.bfloat16), tokens, preferred_element_type=jnp.float32
    ).astype(jnp.bfloat16)
    arrived_input = lax.all_to_all(row_input, "expert", split_axis=0, concat_axis=0, tiled=True)
    inputs_all = lax.all_gather(
        arrived_input.reshape(experts * capacity, width), "dp", axis=0, tiled=True
    )

    col_routes = lax.all_gather(routes, "dp", axis=0, tiled=False)
    col_gates = lax.all_gather(gate_values, "dp", axis=0, tiled=False)
    col_cot = lax.all_gather(cotangent, "dp", axis=0, tiled=False)
    me = lax.axis_index("dp")
    cot_q = lax.dynamic_slice_in_dim(col_cot, me * quarter, quarter, axis=2)
    col_placer, col_slot_gate = jax.vmap(
        lambda r, g: placement(r, g, experts, capacity)
    )(col_routes, col_gates)
    picked_cot = jnp.einsum(
        "gest,gtd->egsd",
        col_placer.astype(jnp.bfloat16),
        cot_q,
        preferred_element_type=jnp.float32,
    )
    row_cot = (jnp.transpose(col_slot_gate, (1, 0, 2))[:, :, :, None] * picked_cot).astype(
        jnp.bfloat16
    )
    arrived_cot = lax.all_to_all(row_cot, "expert", split_axis=0, concat_axis=0, tiled=True)
    cot_quarter = jnp.transpose(arrived_cot, (1, 0, 2, 3)).reshape(
        groups * experts * capacity, quarter
    )

    gate_local = gate_weight[0]
    up_local = up_weight[0]
    down_local = down_weight[0]
    contract_last = (((1,), (1,)), ((), ()))
    gate_pre = lax.dot_general(
        gate_local, inputs_all, contract_last, preferred_element_type=jnp.float32
    )
    up_pre = lax.dot_general(
        up_local, inputs_all, contract_last, preferred_element_type=jnp.float32
    )
    hidden_part = (jax.nn.silu(gate_pre) * up_pre).astype(jnp.bfloat16)
    hidden_all = lax.all_gather(hidden_part, "dp", axis=0, tiled=True)
    contract_lead = (((0,), (0,)), ((), ()))
    expert_out = lax.dot_general(
        hidden_all, down_local, contract_lead, preferred_element_type=jnp.float32
    ).astype(jnp.bfloat16)
    grad_down = jnp.dot(hidden_all, cot_quarter, preferred_element_type=jnp.float32).astype(
        jnp.bfloat16
    )
    grad_hidden = lax.psum_scatter(
        lax.dot_general(down_local, cot_quarter, contract_last, preferred_element_type=jnp.float32),
        "dp",
        scatter_dimension=0,
        tiled=True,
    )
    sigma = jax.nn.sigmoid(gate_pre)
    grad_gate = (grad_hidden * up_pre * sigma * (1.0 + gate_pre * (1.0 - sigma))).astype(
        jnp.bfloat16
    )
    grad_up = (grad_hidden * jax.nn.silu(gate_pre)).astype(jnp.bfloat16)
    grad_gate_local = jnp.dot(grad_gate, inputs_all, preferred_element_type=jnp.float32).astype(
        jnp.bfloat16
    )
    grad_up_local = jnp.dot(grad_up, inputs_all, preferred_element_type=jnp.float32).astype(
        jnp.bfloat16
    )

    out_blocks = jnp.transpose(expert_out.reshape(groups, experts, capacity, quarter), (1, 0, 2, 3))
    returned = lax.all_to_all(out_blocks, "expert", split_axis=0, concat_axis=0, tiled=True)
    combine = col_placer.astype(jnp.float32) * col_slot_gate[:, :, :, None]
    mixed_q = jnp.einsum(
        "gest,egsd->gtd",
        combine,
        returned.astype(jnp.float32),
        precision=lax.Precision.HIGHEST,
        preferred_element_type=jnp.float32,
    ).astype(jnp.bfloat16)
    mixed = lax.all_to_all(mixed_q, "dp", split_axis=0, concat_axis=2, tiled=True)
    return (mixed[0], grad_gate_local[None], grad_up_local[None], grad_down[None])


def solution(mesh):
    in_specs = (
        P(("dp", "expert"), None),
        P(("dp", "expert"), None),
        P(("dp", "expert"), None),
        P(("dp", "expert"), None),
        P("expert", "dp", None),
        P("expert", "dp", None),
        P("expert", None, "dp"),
    )
    out_specs = (
        P(("dp", "expert"), None),
        P("expert", "dp", None),
        P("expert", "dp", None),
        P("expert", None, "dp"),
    )
    return jax.shard_map(body, mesh=mesh, in_specs=in_specs, out_specs=out_specs, check_vma=False)
```

```python
import jax
import jax.numpy as jnp
from jax import lax
from jax.sharding import PartitionSpec as P


def placement(routes, gate_values, experts, capacity):
    onehot = routes[:, :, None] == jnp.arange(experts, dtype=jnp.int32)[None, None, :]
    named = jnp.sum(onehot.astype(jnp.int32), axis=1)
    earlier = jnp.cumsum(named, axis=0) - named
    slot_ids = jnp.arange(capacity, dtype=jnp.int32)[None, :, None]
    placer = (named.T[:, None, :] == 1) & (earlier.T[:, None, :] == slot_ids)
    token_gate = jnp.sum(
        jnp.where(onehot, gate_values[:, :, None], jnp.zeros((), jnp.float32)), axis=1
    )
    slot_gate = jnp.sum(placer.astype(jnp.float32) * token_gate.T[:, None, :], axis=2)
    return placer, slot_gate


def body(tokens, cotangent, routes, gate_values, gate_weight, up_weight, down_weight):
    tok_rows = tokens.shape[0]
    width = tokens.shape[1]
    top_count = routes.shape[1]
    experts = lax.axis_size("expert")
    groups = lax.axis_size("dp")
    quarter = width // groups
    capacity = min(tok_rows, max(2, 2 * tok_rows * top_count // experts))

    placer, _ = placement(routes, gate_values, experts, capacity)
    row_input = jnp.einsum(
        "est,td->esd", placer.astype(jnp.bfloat16), tokens, preferred_element_type=jnp.float32
    ).astype(jnp.bfloat16)
    arrived_input = lax.all_to_all(row_input, "expert", split_axis=0, concat_axis=0, tiled=True)
    inputs_all = lax.all_gather(
        arrived_input.reshape(experts * capacity, width), "dp", axis=0, tiled=True
    )

    packed = jnp.concatenate(
        [cotangent.astype(jnp.float32), routes.astype(jnp.float32), gate_values], axis=1
    )
    col = lax.all_gather(packed, "dp", axis=0, tiled=False)
    col_routes = col[:, :, width:width + top_count].astype(jnp.int32)
    col_gates = col[:, :, width + top_count:]
    me = lax.axis_index("dp")
    cot_q = lax.dynamic_slice_in_dim(col[:, :, :width], me * quarter, quarter, axis=2).astype(
        jnp.bfloat16
    )
    col_placer, col_slot_gate = jax.vmap(
        lambda r, g: placement(r, g, experts, capacity)
    )(col_routes, col_gates)
    picked_cot = jnp.einsum(
        "gest,gtd->egsd",
        col_placer.astype(jnp.bfloat16),
        cot_q,
        preferred_element_type=jnp.float32,
    )
    row_cot = (jnp.transpose(col_slot_gate, (1, 0, 2))[:, :, :, None] * picked_cot).astype(
        jnp.bfloat16
    )
    arrived_cot = lax.all_to_all(row_cot, "expert", split_axis=0, concat_axis=0, tiled=True)
    cot_quarter = jnp.transpose(arrived_cot, (1, 0, 2, 3)).reshape(
        groups * experts * capacity, quarter
    )

    gate_local = gate_weight[0]
    up_local = up_weight[0]
    down_local = down_weight[0]
    contract_last = (((1,), (1,)), ((), ()))
    gate_pre = lax.dot_general(
        gate_local, inputs_all, contract_last, preferred_element_type=jnp.float32
    )
    up_pre = lax.dot_general(
        up_local, inputs_all, contract_last, preferred_element_type=jnp.float32
    )
    hidden_part = (jax.nn.silu(gate_pre) * up_pre).astype(jnp.bfloat16)
    hidden_all = lax.all_gather(hidden_part, "dp", axis=0, tiled=True)
    contract_lead = (((0,), (0,)), ((), ()))
    expert_out = lax.dot_general(
        hidden_all, down_local, contract_lead, preferred_element_type=jnp.float32
    ).astype(jnp.bfloat16)
    grad_down = jnp.dot(hidden_all, cot_quarter, preferred_element_type=jnp.float32).astype(
        jnp.bfloat16
    )
    grad_hidden = lax.psum_scatter(
        lax.dot_general(
            down_local, cot_quarter, contract_last, preferred_element_type=jnp.float32
        ).astype(jnp.bfloat16),
        "dp",
        scatter_dimension=0,
        tiled=True,
    ).astype(jnp.float32)
    sigma = jax.nn.sigmoid(gate_pre)
    grad_gate = (grad_hidden * up_pre * sigma * (1.0 + gate_pre * (1.0 - sigma))).astype(
        jnp.bfloat16
    )
    grad_up = (grad_hidden * jax.nn.silu(gate_pre)).astype(jnp.bfloat16)
    grad_gate_local = jnp.dot(grad_gate, inputs_all, preferred_element_type=jnp.float32).astype(
        jnp.bfloat16
    )
    grad_up_local = jnp.dot(grad_up, inputs_all, preferred_element_type=jnp.float32).astype(
        jnp.bfloat16
    )

    out_blocks = jnp.transpose(expert_out.reshape(groups, experts, capacity, quarter), (1, 0, 2, 3))
    returned = lax.all_to_all(out_blocks, "expert", split_axis=0, concat_axis=0, tiled=True)
    combine = col_placer.astype(jnp.float32) * col_slot_gate[:, :, :, None]
    mixed_q = jnp.einsum(
        "gest,egsd->gtd",
        combine,
        returned.astype(jnp.float32),
        precision=lax.Precision.HIGHEST,
        preferred_element_type=jnp.float32,
    ).astype(jnp.bfloat16)
    mixed = lax.all_to_all(mixed_q, "dp", split_axis=0, concat_axis=2, tiled=True)
    return (mixed[0], grad_gate_local[None], grad_up_local[None], grad_down[None])


def solution(mesh):
    in_specs = (
        P(("dp", "expert"), None),
        P(("dp", "expert"), None),
        P(("dp", "expert"), None),
        P(("dp", "expert"), None),
        P("expert", "dp", None),
        P("expert", "dp", None),
        P("expert", None, "dp"),
    )
    out_specs = (
        P(("dp", "expert"), None),
        P("expert", "dp", None),
        P("expert", "dp", None),
        P("expert", None, "dp"),
    )
    return jax.shard_map(body, mesh=mesh, in_specs=in_specs, out_specs=out_specs, check_vma=False)
```

```python
import jax
import jax.numpy as jnp
from jax import lax
from jax.sharding import PartitionSpec as P


def placement(routes, gate_values, experts, capacity):
    onehot = routes[:, :, None] == jnp.arange(experts, dtype=jnp.int32)[None, None, :]
    named = jnp.sum(onehot.astype(jnp.int32), axis=1)
    earlier = jnp.cumsum(named, axis=0) - named
    slot_ids = jnp.arange(capacity, dtype=jnp.int32)[None, :, None]
    placer = (named.T[:, None, :] == 1) & (earlier.T[:, None, :] == slot_ids)
    token_gate = jnp.sum(
        jnp.where(onehot, gate_values[:, :, None], jnp.zeros((), jnp.float32)), axis=1
    )
    slot_gate = jnp.sum(placer.astype(jnp.float32) * token_gate.T[:, None, :], axis=2)
    return placer, slot_gate


def body(tokens, cotangent, routes, gate_values, gate_weight, up_weight, down_weight):
    tok_rows = tokens.shape[0]
    width = tokens.shape[1]
    top_count = routes.shape[1]
    experts = lax.axis_size("expert")
    groups = lax.axis_size("dp")
    quarter = width // groups
    capacity = min(tok_rows, max(2, 2 * tok_rows * top_count // experts))

    placer, _ = placement(routes, gate_values, experts, capacity)
    row_input = jnp.einsum(
        "est,td->esd", placer.astype(jnp.bfloat16), tokens, preferred_element_type=jnp.float32
    ).astype(jnp.bfloat16)
    inputs_by_slot = []
    for slot in range(capacity):
        arrived_input = lax.all_to_all(
            row_input[:, slot], "expert", split_axis=0, concat_axis=0, tiled=True
        )
        inputs_by_slot.append(lax.all_gather(arrived_input, "dp", axis=0, tiled=True))
    inputs_all = jnp.concatenate(inputs_by_slot, axis=0)

    packed = jnp.concatenate(
        [cotangent.astype(jnp.float32), routes.astype(jnp.float32), gate_values], axis=1
    )
    col = lax.all_gather(packed, "dp", axis=0, tiled=False)
    col_routes = col[:, :, width:width + top_count].astype(jnp.int32)
    col_gates = col[:, :, width + top_count:]
    me = lax.axis_index("dp")
    cot_q = lax.dynamic_slice_in_dim(col[:, :, :width], me * quarter, quarter, axis=2).astype(
        jnp.bfloat16
    )
    col_placer, col_slot_gate = jax.vmap(
        lambda r, g: placement(r, g, experts, capacity)
    )(col_routes, col_gates)
    picked_cot = jnp.einsum(
        "gest,gtd->egsd",
        col_placer.astype(jnp.bfloat16),
        cot_q,
        preferred_element_type=jnp.float32,
    )
    row_cot = (jnp.transpose(col_slot_gate, (1, 0, 2))[:, :, :, None] * picked_cot).astype(
        jnp.bfloat16
    )
    arrived_cot = lax.all_to_all(row_cot, "expert", split_axis=0, concat_axis=0, tiled=True)
    cot_quarter = jnp.transpose(arrived_cot, (2, 1, 0, 3)).reshape(
        groups * experts * capacity, quarter
    )

    gate_local = gate_weight[0]
    up_local = up_weight[0]
    down_local = down_weight[0]
    contract_last = (((1,), (1,)), ((), ()))
    gate_pre = lax.dot_general(
        gate_local, inputs_all, contract_last, preferred_element_type=jnp.float32
    )
    up_pre = lax.dot_general(
        up_local, inputs_all, contract_last, preferred_element_type=jnp.float32
    )
    hidden_part = (jax.nn.silu(gate_pre) * up_pre).astype(jnp.bfloat16)
    hidden_all = lax.all_gather(hidden_part, "dp", axis=0, tiled=True)
    contract_lead = (((0,), (0,)), ((), ()))
    expert_out = lax.dot_general(
        hidden_all, down_local, contract_lead, preferred_element_type=jnp.float32
    ).astype(jnp.bfloat16)
    grad_down = jnp.dot(hidden_all, cot_quarter, preferred_element_type=jnp.float32).astype(
        jnp.bfloat16
    )
    grad_hidden = lax.psum_scatter(
        lax.dot_general(down_local, cot_quarter, contract_last, preferred_element_type=jnp.float32),
        "dp",
        scatter_dimension=0,
        tiled=True,
    )
    sigma = jax.nn.sigmoid(gate_pre)
    grad_gate = (grad_hidden * up_pre * sigma * (1.0 + gate_pre * (1.0 - sigma))).astype(
        jnp.bfloat16
    )
    grad_up = (grad_hidden * jax.nn.silu(gate_pre)).astype(jnp.bfloat16)
    grad_gate_local = jnp.dot(grad_gate, inputs_all, preferred_element_type=jnp.float32).astype(
        jnp.bfloat16
    )
    grad_up_local = jnp.dot(grad_up, inputs_all, preferred_element_type=jnp.float32).astype(
        jnp.bfloat16
    )

    out_blocks = jnp.transpose(expert_out.reshape(capacity, groups, experts, quarter), (2, 1, 0, 3))
    returned = lax.all_to_all(out_blocks, "expert", split_axis=0, concat_axis=0, tiled=True)
    combine = col_placer.astype(jnp.float32) * col_slot_gate[:, :, :, None]
    mixed_q = jnp.einsum(
        "gest,egsd->gtd",
        combine,
        returned.astype(jnp.float32),
        precision=lax.Precision.HIGHEST,
        preferred_element_type=jnp.float32,
    ).astype(jnp.bfloat16)
    mixed = lax.all_to_all(mixed_q, "dp", split_axis=0, concat_axis=2, tiled=True)
    return (mixed[0], grad_gate_local[None], grad_up_local[None], grad_down[None])


def solution(mesh):
    in_specs = (
        P(("dp", "expert"), None),
        P(("dp", "expert"), None),
        P(("dp", "expert"), None),
        P(("dp", "expert"), None),
        P("expert", "dp", None),
        P("expert", "dp", None),
        P("expert", None, "dp"),
    )
    out_specs = (
        P(("dp", "expert"), None),
        P("expert", "dp", None),
        P("expert", "dp", None),
        P("expert", None, "dp"),
    )
    return jax.shard_map(body, mesh=mesh, in_specs=in_specs, out_specs=out_specs, check_vma=False)
```

```python
import jax
import jax.numpy as jnp
from jax import lax
from jax.sharding import PartitionSpec as P


def placement(routes, gate_values, experts, capacity):
    onehot = routes[:, :, None] == jnp.arange(experts, dtype=jnp.int32)[None, None, :]
    named = jnp.sum(onehot.astype(jnp.int32), axis=1)
    earlier = jnp.cumsum(named, axis=0) - named
    slot_ids = jnp.arange(capacity, dtype=jnp.int32)[None, :, None]
    placer = (named.T[:, None, :] == 1) & (earlier.T[:, None, :] == slot_ids)
    token_gate = jnp.sum(
        jnp.where(onehot, gate_values[:, :, None], jnp.zeros((), jnp.float32)), axis=1
    )
    slot_gate = jnp.sum(placer.astype(jnp.float32) * token_gate.T[:, None, :], axis=2)
    return placer, slot_gate


def body(tokens, cotangent, routes, gate_values, gate_weight, up_weight, down_weight):
    tok_rows = tokens.shape[0]
    width = tokens.shape[1]
    top_count = routes.shape[1]
    experts = lax.axis_size("expert")
    groups = lax.axis_size("dp")
    quarter = width // groups
    capacity = min(tok_rows, max(2, 2 * tok_rows * top_count // experts))

    placer, _ = placement(routes, gate_values, experts, capacity)
    row_input = jnp.einsum(
        "est,td->esd", placer.astype(jnp.bfloat16), tokens, preferred_element_type=jnp.float32
    ).astype(jnp.bfloat16)
    arrived_input = lax.all_to_all(row_input, "expert", split_axis=0, concat_axis=0, tiled=True)
    inputs_all = lax.all_gather(
        arrived_input.reshape(experts * capacity, width), "dp", axis=0, tiled=True
    )

    pad = jnp.zeros((tok_rows, 2 * width - 2 * top_count), jnp.float32)
    packed = jnp.concatenate(
        [cotangent.astype(jnp.float32), routes.astype(jnp.float32), gate_values, pad], axis=1
    )
    col = lax.all_gather(packed, "dp", axis=0, tiled=False)
    col_routes = col[:, :, width:width + top_count].astype(jnp.int32)
    col_gates = col[:, :, width + top_count:width + 2 * top_count]
    me = lax.axis_index("dp")
    cot_q = lax.dynamic_slice_in_dim(col[:, :, :width], me * quarter, quarter, axis=2).astype(
        jnp.bfloat16
    )
    col_placer, col_slot_gate = jax.vmap(
        lambda r, g: placement(r, g, experts, capacity)
    )(col_routes, col_gates)
    picked_cot = jnp.einsum(
        "gest,gtd->egsd",
        col_placer.astype(jnp.bfloat16),
        cot_q,
        preferred_element_type=jnp.float32,
    )
    row_cot = (jnp.transpose(col_slot_gate, (1, 0, 2))[:, :, :, None] * picked_cot).astype(
        jnp.bfloat16
    )
    arrived_cot = lax.all_to_all(row_cot, "expert", split_axis=0, concat_axis=0, tiled=True)
    cot_quarter = jnp.transpose(arrived_cot, (1, 0, 2, 3)).reshape(
        groups * experts * capacity, quarter
    )

    gate_local = gate_weight[0]
    up_local = up_weight[0]
    down_local = down_weight[0]
    contract_last = (((1,), (1,)), ((), ()))
    gate_pre = lax.dot_general(
        gate_local, inputs_all, contract_last, preferred_element_type=jnp.float32
    )
    up_pre = lax.dot_general(
        up_local, inputs_all, contract_last, preferred_element_type=jnp.float32
    )
    hidden_part = (jax.nn.silu(gate_pre) * up_pre).astype(jnp.bfloat16)
    hidden_all = lax.all_gather(hidden_part, "dp", axis=0, tiled=True)
    contract_lead = (((0,), (0,)), ((), ()))
    expert_out = lax.dot_general(
        hidden_all, down_local, contract_lead, preferred_element_type=jnp.float32
    ).astype(jnp.bfloat16)
    grad_down = jnp.dot(hidden_all, cot_quarter, preferred_element_type=jnp.float32).astype(
        jnp.bfloat16
    )
    grad_hidden = lax.psum_scatter(
        lax.dot_general(down_local, cot_quarter, contract_last, preferred_element_type=jnp.float32),
        "dp",
        scatter_dimension=0,
        tiled=True,
    )
    sigma = jax.nn.sigmoid(gate_pre)
    grad_gate = (grad_hidden * up_pre * sigma * (1.0 + gate_pre * (1.0 - sigma))).astype(
        jnp.bfloat16
    )
    grad_up = (grad_hidden * jax.nn.silu(gate_pre)).astype(jnp.bfloat16)
    grad_gate_local = jnp.dot(grad_gate, inputs_all, preferred_element_type=jnp.float32).astype(
        jnp.bfloat16
    )
    grad_up_local = jnp.dot(grad_up, inputs_all, preferred_element_type=jnp.float32).astype(
        jnp.bfloat16
    )

    out_blocks = jnp.transpose(expert_out.reshape(groups, experts, capacity, quarter), (1, 0, 2, 3))
    returned = lax.all_to_all(out_blocks, "expert", split_axis=0, concat_axis=0, tiled=True)
    combine = col_placer.astype(jnp.float32) * col_slot_gate[:, :, :, None]
    mixed_q = jnp.einsum(
        "gest,egsd->gtd",
        combine,
        returned.astype(jnp.float32),
        precision=lax.Precision.HIGHEST,
        preferred_element_type=jnp.float32,
    ).astype(jnp.bfloat16)
    mixed = lax.all_to_all(mixed_q, "dp", split_axis=0, concat_axis=2, tiled=True)
    return (mixed[0], grad_gate_local[None], grad_up_local[None], grad_down[None])


def solution(mesh):
    in_specs = (
        P(("dp", "expert"), None),
        P(("dp", "expert"), None),
        P(("dp", "expert"), None),
        P(("dp", "expert"), None),
        P("expert", "dp", None),
        P("expert", "dp", None),
        P("expert", None, "dp"),
    )
    out_specs = (
        P(("dp", "expert"), None),
        P("expert", "dp", None),
        P("expert", "dp", None),
        P("expert", None, "dp"),
    )
    return jax.shard_map(body, mesh=mesh, in_specs=in_specs, out_specs=out_specs, check_vma=False)
```

```python
import jax
import jax.numpy as jnp
from jax import lax
from jax.sharding import PartitionSpec as P


def placement(routes, gate_values, experts, capacity):
    onehot = routes[:, :, None] == jnp.arange(experts, dtype=jnp.int32)[None, None, :]
    named = jnp.sum(onehot.astype(jnp.int32), axis=1)
    earlier = jnp.cumsum(named, axis=0) - named
    slot_ids = jnp.arange(capacity, dtype=jnp.int32)[None, :, None]
    placer = (named.T[:, None, :] == 1) & (earlier.T[:, None, :] == slot_ids)
    token_gate = jnp.sum(
        jnp.where(onehot, gate_values[:, :, None], jnp.zeros((), jnp.float32)), axis=1
    )
    slot_gate = jnp.sum(placer.astype(jnp.float32) * token_gate.T[:, None, :], axis=2)
    return placer, slot_gate


def body(tokens, cotangent, routes, gate_values, gate_weight, up_weight, down_weight):
    tok_rows = tokens.shape[0]
    width = tokens.shape[1]
    top_count = routes.shape[1]
    experts = lax.axis_size("expert")
    groups = lax.axis_size("dp")
    quarter = width // groups
    capacity = min(tok_rows, max(2, 2 * tok_rows * top_count // experts))

    placer, _ = placement(routes, gate_values, experts, capacity)
    row_input = jnp.einsum(
        "est,td->esd", placer.astype(jnp.bfloat16), tokens, preferred_element_type=jnp.float32
    ).astype(jnp.bfloat16)
    arrived_input = lax.all_to_all(row_input, "expert", split_axis=0, concat_axis=0, tiled=True)
    inputs_all = lax.all_gather(
        arrived_input.reshape(experts * capacity, width), "dp", axis=0, tiled=True
    )

    col_routes = lax.all_gather(routes, "dp", axis=0, tiled=False)
    col_gates = lax.all_gather(gate_values, "dp", axis=0, tiled=False)
    col_cot = lax.all_gather(cotangent, "dp", axis=0, tiled=False)
    me = lax.axis_index("dp")
    cot_q = lax.dynamic_slice_in_dim(col_cot, me * quarter, quarter, axis=2)
    col_placer, col_slot_gate = jax.vmap(
        lambda r, g: placement(r, g, experts, capacity)
    )(col_routes, col_gates)
    picked_cot = jnp.einsum(
        "gest,gtd->egsd",
        col_placer.astype(jnp.bfloat16),
        cot_q,
        preferred_element_type=jnp.float32,
    )
    row_cot = (jnp.transpose(col_slot_gate, (1, 0, 2))[:, :, :, None] * picked_cot).astype(
        jnp.bfloat16
    )
    arrived_cot = lax.all_to_all(row_cot, "expert", split_axis=0, concat_axis=0, tiled=True)
    cot_quarter = jnp.transpose(arrived_cot, (1, 0, 2, 3)).reshape(
        groups * experts * capacity, quarter
    )

    gate_local = gate_weight[0]
    up_local = up_weight[0]
    down_local = down_weight[0]
    contract_last = (((1,), (1,)), ((), ()))
    gate_pre = lax.dot_general(
        gate_local, inputs_all, contract_last, preferred_element_type=jnp.float32
    )
    up_pre = lax.dot_general(
        up_local, inputs_all, contract_last, preferred_element_type=jnp.float32
    )
    hidden_part = (jax.nn.silu(gate_pre) * up_pre).astype(jnp.bfloat16)
    hidden_copies = jnp.broadcast_to(hidden_part[None], (groups,) + hidden_part.shape)
    hidden_all = lax.all_to_all(hidden_copies, "dp", split_axis=0, concat_axis=0, tiled=True).reshape(
        groups * hidden_part.shape[0], hidden_part.shape[1]
    )
    contract_lead = (((0,), (0,)), ((), ()))
    expert_out = lax.dot_general(
        hidden_all, down_local, contract_lead, preferred_element_type=jnp.float32
    ).astype(jnp.bfloat16)
    grad_down = jnp.dot(hidden_all, cot_quarter, preferred_element_type=jnp.float32).astype(
        jnp.bfloat16
    )
    grad_hidden = lax.psum_scatter(
        lax.dot_general(down_local, cot_quarter, contract_last, preferred_element_type=jnp.float32),
        "dp",
        scatter_dimension=0,
        tiled=True,
    )
    sigma = jax.nn.sigmoid(gate_pre)
    grad_gate = (grad_hidden * up_pre * sigma * (1.0 + gate_pre * (1.0 - sigma))).astype(
        jnp.bfloat16
    )
    grad_up = (grad_hidden * jax.nn.silu(gate_pre)).astype(jnp.bfloat16)
    grad_gate_local = jnp.dot(grad_gate, inputs_all, preferred_element_type=jnp.float32).astype(
        jnp.bfloat16
    )
    grad_up_local = jnp.dot(grad_up, inputs_all, preferred_element_type=jnp.float32).astype(
        jnp.bfloat16
    )

    out_blocks = jnp.transpose(expert_out.reshape(groups, experts, capacity, quarter), (1, 0, 2, 3))
    returned = lax.all_to_all(out_blocks, "expert", split_axis=0, concat_axis=0, tiled=True)
    combine = col_placer.astype(jnp.float32) * col_slot_gate[:, :, :, None]
    mixed_q = jnp.einsum(
        "gest,egsd->gtd",
        combine,
        returned.astype(jnp.float32),
        precision=lax.Precision.HIGHEST,
        preferred_element_type=jnp.float32,
    ).astype(jnp.bfloat16)
    mixed = lax.all_to_all(mixed_q, "dp", split_axis=0, concat_axis=2, tiled=True)
    return (mixed[0], grad_gate_local[None], grad_up_local[None], grad_down[None])


def solution(mesh):
    in_specs = (
        P(("dp", "expert"), None),
        P(("dp", "expert"), None),
        P(("dp", "expert"), None),
        P(("dp", "expert"), None),
        P("expert", "dp", None),
        P("expert", "dp", None),
        P("expert", None, "dp"),
    )
    out_specs = (
        P(("dp", "expert"), None),
        P("expert", "dp", None),
        P("expert", "dp", None),
        P("expert", None, "dp"),
    )
    return jax.shard_map(body, mesh=mesh, in_specs=in_specs, out_specs=out_specs, check_vma=False)
```

```python
import jax
import jax.numpy as jnp
from jax import lax
from jax.sharding import PartitionSpec as P


def placement(routes, gate_values, experts, capacity):
    onehot = routes[:, :, None] == jnp.arange(experts, dtype=jnp.int32)[None, None, :]
    named = jnp.sum(onehot.astype(jnp.int32), axis=1)
    earlier = jnp.cumsum(named, axis=0) - named
    slot_ids = jnp.arange(capacity, dtype=jnp.int32)[None, :, None]
    placer = (named.T[:, None, :] == 1) & (earlier.T[:, None, :] == slot_ids)
    token_gate = jnp.sum(
        jnp.where(onehot, gate_values[:, :, None], jnp.zeros((), jnp.float32)), axis=1
    )
    slot_gate = jnp.sum(placer.astype(jnp.float32) * token_gate.T[:, None, :], axis=2)
    return placer, slot_gate


def body(tokens, cotangent, routes, gate_values, gate_weight, up_weight, down_weight):
    tok_rows = tokens.shape[0]
    width = tokens.shape[1]
    top_count = routes.shape[1]
    experts = lax.axis_size("expert")
    groups = lax.axis_size("dp")
    quarter = width // groups
    capacity = min(tok_rows, max(2, 2 * tok_rows * top_count // experts))

    placer, _ = placement(routes, gate_values, experts, capacity)
    row_input = jnp.einsum(
        "est,td->esd", placer.astype(jnp.bfloat16), tokens, preferred_element_type=jnp.float32
    ).astype(jnp.bfloat16)
    arrived_input = lax.all_to_all(row_input, "expert", split_axis=0, concat_axis=0, tiled=True)
    inputs_all = lax.all_gather(
        arrived_input.reshape(experts * capacity, width), "dp", axis=0, tiled=True
    )

    col_routes = lax.all_gather(routes, "dp", axis=0, tiled=False)
    col_gates = lax.all_gather(gate_values, "dp", axis=0, tiled=False)
    col_cot = lax.all_gather(cotangent, "dp", axis=0, tiled=False)
    me = lax.axis_index("dp")
    cot_q = lax.dynamic_slice_in_dim(col_cot, me * quarter, quarter, axis=2)
    col_placer, col_slot_gate = jax.vmap(
        lambda r, g: placement(r, g, experts, capacity)
    )(col_routes, col_gates)
    picked_cot = jnp.einsum(
        "gest,gtd->egsd",
        col_placer.astype(jnp.bfloat16),
        cot_q,
        preferred_element_type=jnp.float32,
    )
    row_cot = (jnp.transpose(col_slot_gate, (1, 0, 2))[:, :, :, None] * picked_cot).astype(
        jnp.bfloat16
    )
    arrived_cot = lax.all_to_all(row_cot, "expert", split_axis=0, concat_axis=0, tiled=True)
    cot_quarter = jnp.transpose(arrived_cot, (1, 0, 2, 3)).reshape(
        groups * experts * capacity, quarter
    )

    gate_local = gate_weight[0]
    up_local = up_weight[0]
    down_local = down_weight[0]
    contract_last = (((1,), (1,)), ((), ()))
    gate_pre = lax.dot_general(
        gate_local, inputs_all, contract_last, preferred_element_type=jnp.float32
    )
    up_pre = lax.dot_general(
        up_local, inputs_all, contract_last, preferred_element_type=jnp.float32
    )
    hidden_part = (jax.nn.silu(gate_pre) * up_pre).astype(jnp.bfloat16)
    hidden_all = lax.all_gather(hidden_part, "dp", axis=0, tiled=True)
    contract_lead = (((0,), (0,)), ((), ()))
    expert_out = lax.dot_general(
        hidden_all, down_local, contract_lead, preferred_element_type=jnp.float32
    ).astype(jnp.bfloat16)
    grad_down = jnp.dot(hidden_all, cot_quarter, preferred_element_type=jnp.float32).astype(
        jnp.bfloat16
    )
    grad_hidden = lax.psum_scatter(
        lax.dot_general(down_local, cot_quarter, contract_last, preferred_element_type=jnp.float32),
        "dp",
        scatter_dimension=0,
        tiled=True,
    )
    out_blocks = jnp.transpose(expert_out.reshape(groups, experts, capacity, quarter), (1, 0, 2, 3))
    returned = lax.all_to_all(out_blocks, "expert", split_axis=0, concat_axis=0, tiled=True)
    combine = col_placer.astype(jnp.float32) * col_slot_gate[:, :, :, None]
    mixed_q = jnp.einsum(
        "gest,egsd->gtd",
        combine,
        returned.astype(jnp.float32),
        precision=lax.Precision.HIGHEST,
        preferred_element_type=jnp.float32,
    ).astype(jnp.bfloat16)
    grad_hidden, mixed_q = lax.optimization_barrier((grad_hidden, mixed_q))
    sigma = jax.nn.sigmoid(gate_pre)
    grad_gate = (grad_hidden * up_pre * sigma * (1.0 + gate_pre * (1.0 - sigma))).astype(
        jnp.bfloat16
    )
    grad_up = (grad_hidden * jax.nn.silu(gate_pre)).astype(jnp.bfloat16)
    grad_gate_local = jnp.dot(grad_gate, inputs_all, preferred_element_type=jnp.float32).astype(
        jnp.bfloat16
    )
    grad_up_local = jnp.dot(grad_up, inputs_all, preferred_element_type=jnp.float32).astype(
        jnp.bfloat16
    )

    mixed = lax.all_to_all(mixed_q, "dp", split_axis=0, concat_axis=2, tiled=True)
    return (mixed[0], grad_gate_local[None], grad_up_local[None], grad_down[None])


def solution(mesh):
    in_specs = (
        P(("dp", "expert"), None),
        P(("dp", "expert"), None),
        P(("dp", "expert"), None),
        P(("dp", "expert"), None),
        P("expert", "dp", None),
        P("expert", "dp", None),
        P("expert", None, "dp"),
    )
    out_specs = (
        P(("dp", "expert"), None),
        P("expert", "dp", None),
        P("expert", "dp", None),
        P("expert", None, "dp"),
    )
    return jax.shard_map(body, mesh=mesh, in_specs=in_specs, out_specs=out_specs, check_vma=False)
```

```python
import jax
import jax.numpy as jnp
from jax import lax
from jax.sharding import PartitionSpec as P


def placement(routes, gate_values, experts, capacity):
    onehot = routes[:, :, None] == jnp.arange(experts, dtype=jnp.int32)[None, None, :]
    named = jnp.sum(onehot.astype(jnp.int32), axis=1)
    earlier = jnp.cumsum(named, axis=0) - named
    slot_ids = jnp.arange(capacity, dtype=jnp.int32)[None, :, None]
    placer = (named.T[:, None, :] == 1) & (earlier.T[:, None, :] == slot_ids)
    token_gate = jnp.sum(
        jnp.where(onehot, gate_values[:, :, None], jnp.zeros((), jnp.float32)), axis=1
    )
    slot_gate = jnp.sum(placer.astype(jnp.float32) * token_gate.T[:, None, :], axis=2)
    return placer, slot_gate


def body(tokens, cotangent, routes, gate_values, gate_weight, up_weight, down_weight):
    tok_rows = tokens.shape[0]
    width = tokens.shape[1]
    top_count = routes.shape[1]
    experts = lax.axis_size("expert")
    groups = lax.axis_size("dp")
    quarter = width // groups
    capacity = min(tok_rows, max(2, 2 * tok_rows * top_count // experts))

    placer, _ = placement(routes, gate_values, experts, capacity)
    row_input = jnp.einsum(
        "est,td->esd", placer.astype(jnp.bfloat16), tokens, preferred_element_type=jnp.float32
    ).astype(jnp.bfloat16)
    arrived_input = lax.all_to_all(row_input, "expert", split_axis=0, concat_axis=0, tiled=True)
    inputs_all = lax.all_gather(
        arrived_input.reshape(experts * capacity, width), "dp", axis=0, tiled=True
    )

    col_routes = lax.all_gather(routes, "dp", axis=0, tiled=False)
    col_gates = lax.all_gather(gate_values, "dp", axis=0, tiled=False)
    col_cot = lax.all_gather(cotangent, "dp", axis=0, tiled=False)
    me = lax.axis_index("dp")
    cot_q = lax.dynamic_slice_in_dim(col_cot, me * quarter, quarter, axis=2)
    col_placer, col_slot_gate = jax.vmap(
        lambda r, g: placement(r, g, experts, capacity)
    )(col_routes, col_gates)
    picked_cot = jnp.einsum(
        "gest,gtd->egsd",
        col_placer.astype(jnp.bfloat16),
        cot_q,
        preferred_element_type=jnp.float32,
    )
    row_cot = (jnp.transpose(col_slot_gate, (1, 0, 2))[:, :, :, None] * picked_cot).astype(
        jnp.bfloat16
    )
    arrived_cot = lax.all_to_all(row_cot, "expert", split_axis=0, concat_axis=0, tiled=True)
    cot_quarter = jnp.transpose(arrived_cot, (1, 0, 2, 3)).reshape(
        groups * experts * capacity, quarter
    )

    gate_local = gate_weight[0]
    up_local = up_weight[0]
    down_local = down_weight[0]
    contract_last = (((1,), (1,)), ((), ()))
    gate_pre = lax.dot_general(
        gate_local, inputs_all, contract_last, preferred_element_type=jnp.float32
    )
    up_pre = lax.dot_general(
        up_local, inputs_all, contract_last, preferred_element_type=jnp.float32
    )
    hidden_part = (jax.nn.silu(gate_pre) * up_pre).astype(jnp.bfloat16)
    hidden_all = lax.all_gather(hidden_part, "dp", axis=0, tiled=True)
    contract_lead = (((0,), (0,)), ((), ()))
    expert_out = lax.dot_general(
        hidden_all, down_local, contract_lead, preferred_element_type=jnp.float32
    ).astype(jnp.bfloat16)
    grad_down = jnp.dot(hidden_all, cot_quarter, preferred_element_type=jnp.float32).astype(
        jnp.bfloat16
    )
    grad_hidden = lax.psum_scatter(
        lax.dot_general(down_local, cot_quarter, contract_last, preferred_element_type=jnp.float32),
        "dp",
        scatter_dimension=0,
        tiled=True,
    )
    sigma = jax.nn.sigmoid(gate_pre)
    grad_gate = (grad_hidden * up_pre * sigma * (1.0 + gate_pre * (1.0 - sigma))).astype(
        jnp.bfloat16
    )
    grad_up = (grad_hidden * jax.nn.silu(gate_pre)).astype(jnp.bfloat16)
    grad_gate_local = jnp.dot(grad_gate, inputs_all, preferred_element_type=jnp.float32).astype(
        jnp.bfloat16
    )
    grad_up_local = jnp.dot(grad_up, inputs_all, preferred_element_type=jnp.float32).astype(
        jnp.bfloat16
    )

    out_blocks = jnp.transpose(expert_out.reshape(groups, experts, capacity, quarter), (1, 0, 2, 3))
    out_blocks, grad_down = lax.optimization_barrier((out_blocks, grad_down))
    returned = lax.all_to_all(out_blocks, "expert", split_axis=0, concat_axis=0, tiled=True)
    combine = col_placer.astype(jnp.float32) * col_slot_gate[:, :, :, None]
    mixed_q = jnp.einsum(
        "gest,egsd->gtd",
        combine,
        returned.astype(jnp.float32),
        precision=lax.Precision.HIGHEST,
        preferred_element_type=jnp.float32,
    ).astype(jnp.bfloat16)
    mixed = lax.all_to_all(mixed_q, "dp", split_axis=0, concat_axis=2, tiled=True)
    return (mixed[0], grad_gate_local[None], grad_up_local[None], grad_down[None])


def solution(mesh):
    in_specs = (
        P(("dp", "expert"), None),
        P(("dp", "expert"), None),
        P(("dp", "expert"), None),
        P(("dp", "expert"), None),
        P("expert", "dp", None),
        P("expert", "dp", None),
        P("expert", None, "dp"),
    )
    out_specs = (
        P(("dp", "expert"), None),
        P("expert", "dp", None),
        P("expert", "dp", None),
        P("expert", None, "dp"),
    )
    return jax.shard_map(body, mesh=mesh, in_specs=in_specs, out_specs=out_specs, check_vma=False)
```

```python
import jax
import jax.numpy as jnp
from jax import lax
from jax.sharding import PartitionSpec as P


def placement(routes, gate_values, experts, capacity):
    onehot = routes[:, :, None] == jnp.arange(experts, dtype=jnp.int32)[None, None, :]
    named = jnp.sum(onehot.astype(jnp.int32), axis=1)
    earlier = jnp.cumsum(named, axis=0) - named
    slot_ids = jnp.arange(capacity, dtype=jnp.int32)[None, :, None]
    placer = (named.T[:, None, :] == 1) & (earlier.T[:, None, :] == slot_ids)
    token_gate = jnp.sum(
        jnp.where(onehot, gate_values[:, :, None], jnp.zeros((), jnp.float32)), axis=1
    )
    slot_gate = jnp.sum(placer.astype(jnp.float32) * token_gate.T[:, None, :], axis=2)
    return placer, slot_gate


def body(tokens, cotangent, routes, gate_values, gate_weight, up_weight, down_weight):
    tok_rows = tokens.shape[0]
    width = tokens.shape[1]
    top_count = routes.shape[1]
    experts = lax.axis_size("expert")
    groups = lax.axis_size("dp")
    quarter = width // groups
    capacity = min(tok_rows, max(2, 2 * tok_rows * top_count // experts))

    placer, _ = placement(routes, gate_values, experts, capacity)
    row_input = jnp.einsum(
        "est,td->esd", placer.astype(jnp.bfloat16), tokens, preferred_element_type=jnp.float32
    ).astype(jnp.bfloat16)
    arrived_input = lax.all_to_all(row_input, "expert", split_axis=0, concat_axis=0, tiled=True)
    inputs_all = lax.all_gather(
        arrived_input.reshape(experts * capacity, width), "dp", axis=0, tiled=True
    )

    col_meta = lax.all_gather(
        jnp.concatenate([routes.astype(jnp.float32), gate_values], axis=1), "dp", axis=0, tiled=False
    )
    col_routes = col_meta[:, :, :top_count].astype(jnp.int32)
    col_gates = col_meta[:, :, top_count:]
    col_cot = lax.all_gather(cotangent, "dp", axis=0, tiled=False)
    me = lax.axis_index("dp")
    cot_q = lax.dynamic_slice_in_dim(col_cot, me * quarter, quarter, axis=2)
    col_placer, col_slot_gate = jax.vmap(
        lambda r, g: placement(r, g, experts, capacity)
    )(col_routes, col_gates)
    picked_cot = jnp.einsum(
        "gest,gtd->egsd",
        col_placer.astype(jnp.bfloat16),
        cot_q,
        preferred_element_type=jnp.float32,
    )
    row_cot = (jnp.transpose(col_slot_gate, (1, 0, 2))[:, :, :, None] * picked_cot).astype(
        jnp.bfloat16
    )
    arrived_cot = lax.all_to_all(row_cot, "expert", split_axis=0, concat_axis=0, tiled=True)
    cot_quarter = jnp.transpose(arrived_cot, (1, 0, 2, 3)).reshape(
        groups * experts * capacity, quarter
    )

    gate_local = gate_weight[0]
    up_local = up_weight[0]
    down_local = down_weight[0]
    contract_last = (((1,), (1,)), ((), ()))
    gate_pre = lax.dot_general(
        gate_local, inputs_all, contract_last, preferred_element_type=jnp.float32
    )
    up_pre = lax.dot_general(
        up_local, inputs_all, contract_last, preferred_element_type=jnp.float32
    )
    hidden_part = (jax.nn.silu(gate_pre) * up_pre).astype(jnp.bfloat16)
    hidden_all = lax.all_gather(hidden_part, "dp", axis=0, tiled=True)
    contract_lead = (((0,), (0,)), ((), ()))
    expert_out = lax.dot_general(
        hidden_all, down_local, contract_lead, preferred_element_type=jnp.float32
    ).astype(jnp.bfloat16)
    grad_down = jnp.dot(hidden_all, cot_quarter, preferred_element_type=jnp.float32).astype(
        jnp.bfloat16
    )
    grad_hidden = lax.psum_scatter(
        lax.dot_general(down_local, cot_quarter, contract_last, preferred_element_type=jnp.float32),
        "dp",
        scatter_dimension=0,
        tiled=True,
    )
    sigma = jax.nn.sigmoid(gate_pre)
    grad_gate = (grad_hidden * up_pre * sigma * (1.0 + gate_pre * (1.0 - sigma))).astype(
        jnp.bfloat16
    )
    grad_up = (grad_hidden * jax.nn.silu(gate_pre)).astype(jnp.bfloat16)
    grad_gate_local = jnp.dot(grad_gate, inputs_all, preferred_element_type=jnp.float32).astype(
        jnp.bfloat16
    )
    grad_up_local = jnp.dot(grad_up, inputs_all, preferred_element_type=jnp.float32).astype(
        jnp.bfloat16
    )

    out_blocks = jnp.transpose(expert_out.reshape(groups, experts, capacity, quarter), (1, 0, 2, 3))
    returned = lax.all_to_all(out_blocks, "expert", split_axis=0, concat_axis=0, tiled=True)
    combine = col_placer.astype(jnp.float32) * col_slot_gate[:, :, :, None]
    mixed_q = jnp.einsum(
        "gest,egsd->gtd",
        combine,
        returned.astype(jnp.float32),
        precision=lax.Precision.HIGHEST,
        preferred_element_type=jnp.float32,
    ).astype(jnp.bfloat16)
    mixed = lax.all_to_all(mixed_q, "dp", split_axis=0, concat_axis=2, tiled=True)
    return (mixed[0], grad_gate_local[None], grad_up_local[None], grad_down[None])


def solution(mesh):
    in_specs = (
        P(("dp", "expert"), None),
        P(("dp", "expert"), None),
        P(("dp", "expert"), None),
        P(("dp", "expert"), None),
        P("expert", "dp", None),
        P("expert", "dp", None),
        P("expert", None, "dp"),
    )
    out_specs = (
        P(("dp", "expert"), None),
        P("expert", "dp", None),
        P("expert", "dp", None),
        P("expert", None, "dp"),
    )
    return jax.shard_map(body, mesh=mesh, in_specs=in_specs, out_specs=out_specs, check_vma=False)
```
